32 devices in a mesh: row: 4 (over z), col: 8 (over y, x, core).
Axes of the slice: x: 2, y: 2, z: 4, core: 2. Of those that a mesh axis runs over, the one named last changes fastest.
Arguments:
- amplitudes: float32 [1024, 8192], P('col', 'row'), may hold values from -6 to 6
- integrals: float32 [8192, 32768], P('row', 'col'), may hold values from -0.0625 to 0.0625
- integral_mask: int32 [64, 256], P('row', 'col'), may hold values 0 or 1
- denominators: float32 [1024, 32768], P('row', 'col'), may hold values from 0.25 to 2
- cycle_tiles: float32 [32768, 512], P('col'), may hold values from -0.25 to 0.25
- cycle_mask: int32 [256, 4], P('col'), may hold values 0 or 1
- destination: int32 [1024, 256], P('row', 'col'), may hold values from 0 to 262143, as said below
Outputs:
- update: float32 [1024, 32768], P('row', 'col')
- cycle_term: float32 [1024, 32768], P('row', 'col')
The draws below stay inside these ranges and needn't reach their ends.
Inputs may be any that keep to these rules, and one draw needn't show every extreme that they name: destination is a permutation of the units. Numbering a unit (r, t) as r * 256 + t and cutting the units into blocks of 256 rows by 32 tiles, every block sends exactly 256 of its units to every block.
All inputs are finite; a program needn't handle non-finite values. No bound on the sum of `integral_mask` or of `cycle_mask` on one device may be relied on, other than what follows from the above.
Results may differ from the reference program's by a relative error of at most 0.0003.
Values sent between devices are 32-bit elements; how exact they have to be, the bound alone decides.
A program may use at most 192 MiB of HBM per device.

```python
import math
import jax
import jax.numpy as jnp
from jax import lax

V2 = 32768
TILE = 128
RB = 512
OCC = 1024
VT = 256
CD = 8192
IJ_DEV = 256
TPD = 32
CAP = 256


def draw_destination(key, part):
    base = jax.random.fold_in(key, 7)
    key_src, key_dst = jax.random.split(base)
    units = IJ_DEV * TPD
    row_blocks = OCC // IJ_DEV
    col_blocks = VT // TPD
    ndev = row_blocks * col_blocks
    src_perm = jax.vmap(lambda k: jax.random.permutation(k, units))(jax.random.split(key_src, ndev)).astype(jnp.int32)
    dst_perm = jax.vmap(lambda k: jax.random.permutation(k, units))(jax.random.split(key_dst, ndev)).astype(jnp.int32)
    dvec = jnp.arange(ndev, dtype=jnp.int32)[:, None, None]
    svec = jnp.arange(ndev, dtype=jnp.int32)[None, :, None]
    kvec = jnp.arange(CAP, dtype=jnp.int32)[None, None, :]
    slot = dst_perm[dvec, svec * CAP + kvec]
    local = src_perm[svec, dvec * CAP + kvec]

    def global_unit(device, loc):
        prow = device // col_blocks
        pcol = device % col_blocks
        return (prow * IJ_DEV + loc // TPD) * VT + pcol * TPD + loc % TPD
    out_q = global_unit(jnp.broadcast_to(dvec, slot.shape), slot)
    in_q = global_unit(jnp.broadcast_to(svec, local.shape), local)
    dest = jnp.zeros((OCC * VT,), jnp.int32).at[in_q.reshape(-1)].set(out_q.reshape(-1))
    return dest.reshape(OCC, VT)


def touch_ends(values, own_key, smallest, top_value):
    shape = values.shape
    spot = [jax.random.randint(jax.random.fold_in(own_key, axis), (), 0, shape[axis]) for axis in range(len(shape))]
    values = values.at[tuple(spot)].set(smallest)
    longest = shape.index(max(shape))
    spot[longest] = (spot[longest] + 1) % shape[longest]
    return values.at[tuple(spot)].set(top_value)


def level_of(rng, dims, cuts, low, largest):
    def one(axis_at, parts):
        draws = jax.random.uniform(jax.random.fold_in(jax.random.fold_in(rng, 6), axis_at), (parts,), jnp.float32, low / len(cuts), largest / len(cuts))
        return jnp.repeat(jnp.exp(draws), dims[axis_at] // parts).reshape((-1,) + (1,) * (len(dims) - axis_at - 1))

    loudness = one(*cuts[0])
    for cut in cuts[1:]:
        loudness = loudness * one(*cut)
    return loudness


def gaussian(rng, dims, deviation, most, cuts=(), kind=jnp.bfloat16):
    level = level_of(rng, dims, cuts, -0.22, 0.18) if cuts else 1.0
    array = jax.random.normal(rng, dims, jnp.float32) * deviation * level
    return jnp.minimum(jnp.maximum(array, -most), most).astype(kind)


def setup_inputs(seed: int = 0) -> dict:
    key_list = jax.random.split(jax.random.key(seed), 8)
    return {
        "amplitudes": gaussian(key_list[0], (OCC, CD), 1.0, 6.0, ((0, 8), (1, 4)), jnp.float32),
        "integrals": gaussian(key_list[1], (CD, V2), CD ** -0.5, 0.0625, ((0, 4), (1, 8)), jnp.float32),
        "integral_mask": touch_ends((jax.random.randint(key_list[2], (CD // TILE, VT), 0, 5) < 3).astype(jnp.int32), jax.random.fold_in(key_list[2], 1), 0, 1),
        "denominators": jnp.clip(jnp.exp(math.log(2.0) - 2.0794415 * jax.random.uniform(key_list[3], (OCC, V2), jnp.float32) ** level_of(key_list[3], (OCC, V2), ((0, 4), (1, 8)), -0.2, 0.2)), 0.25, 2.0),
        "cycle_tiles": gaussian(key_list[4], (V2, RB), RB ** -0.5, 0.25, ((0, 8),), jnp.float32),
        "cycle_mask": touch_ends((jax.random.randint(key_list[5], (VT, RB // TILE), 0, 5) < 3).astype(jnp.int32), jax.random.fold_in(key_list[5], 1), 0, 1),
        "destination": draw_destination(jax.random.fold_in(key_list[7], 71), 0),
    }


def reference(amplitudes, integrals, integral_mask, denominators, cycle_tiles, cycle_mask, destination):
    width = V2 // 16
    tiles_blk = width // TILE
    mask_f = integral_mask.astype(jnp.float32)

    def column_block(index):
        start = (index * width).astype(jnp.int32)
        block = lax.dynamic_slice_in_dim(integrals, start, width, 1)
        mblock = lax.dynamic_slice_in_dim(mask_f, (index * tiles_blk).astype(jnp.int32), tiles_blk, 1)
        masked = (block.reshape(CD // TILE, TILE, tiles_blk, TILE) * mblock[:, None, :, None]).reshape(CD, width)
        return jnp.dot(amplitudes, masked, precision=lax.Precision.HIGHEST, preferred_element_type=jnp.float32)

    blocks = lax.map(column_block, jnp.arange(16, dtype=jnp.int32))
    residual = jnp.transpose(blocks, (1, 0, 2)).reshape(OCC, V2)
    units = residual.reshape(OCC * VT, TILE)
    moved = jnp.zeros_like(units).at[destination.reshape(-1)].set(units).reshape(OCC, V2)
    update = moved / denominators
    rmask = cycle_mask.astype(jnp.float32)
    cycle = (cycle_tiles.reshape(VT, TILE, RB // TILE, TILE) * rmask[:, None, :, None]).reshape(V2 // RB, RB, RB)
    cycle_term = jnp.einsum("okr,krs->oks", update.reshape(OCC, V2 // RB, RB), cycle,
                           precision=lax.Precision.HIGHEST, preferred_element_type=jnp.float32).reshape(OCC, V2)
    return update, cycle_term
```

```python
import functools
import jax
import jax.numpy as jnp
from jax import lax
from jax.experimental import pallas as pl
from jax.experimental.pallas import tpu as pltpu
from jax.sharding import PartitionSpec as P

TILE = 128
F32 = jnp.float32
BF16 = jnp.bfloat16
CHUNKS = 4


def split(x):
    hi = x.astype(BF16)
    return hi, (x - hi.astype(F32)).astype(BF16)


def dot(a, b):
    return jnp.dot(a, b, preferred_element_type=F32)


def product_kernel(nblk, first_tile, tpb, off_ref, mask_ref, a_ref, b_ref, *rest):
    outs, (a_hi, a_lo, b_hi, b_lo) = rest[:-4], rest[-4:]
    rows, depth = a_ref.shape
    blk = rows // nblk
    step = pl.program_id(0)

    @pl.when(step == 0)
    def _():
        for j in range(nblk):
            src = pl.multiple_of(off_ref[j] * blk, blk)
            hi, lo = split(a_ref[pl.ds(src, blk), :])
            a_hi[pl.ds(j * blk, blk), :] = hi
            a_lo[pl.ds(j * blk, blk), :] = lo

    @pl.loop(0, depth // TILE)
    def _(c):
        at = pl.ds(pl.multiple_of(c * TILE, TILE), TILE)
        for t in range(tpb):
            cols = pl.ds(t * TILE, TILE)
            m = mask_ref[c, first_tile + step * tpb + t].astype(F32)
            hi, lo = split(b_ref[at, cols] * m)
            b_hi[at, cols] = hi
            b_lo[at, cols] = lo

    big = rows // 2
    piece = rows // len(outs)
    per = big // piece if big >= piece else 1
    for h in range(2):
        at = pl.ds(h * big, big)
        acc = dot(a_hi[at, :], b_hi[...]) + dot(a_lo[at, :], b_hi[...]) + dot(a_hi[at, :], b_lo[...])
        for t in range(tpb):
            col = acc[:, t * TILE:(t + 1) * TILE]
            if len(outs) == 1:
                outs[0][t, at, :] = col
            else:
                for q in range(per):
                    outs[h * per + q][t, :, :] = col[q * piece:(q + 1) * piece]


def product(amps, integrals, mask, offsets, chunk, nblk, npieces):
    rows, depth = amps.shape
    cols = integrals.shape[1]
    width = cols // CHUNKS
    tpb = min(4, width // TILE)
    bn = tpb * TILE
    steps = width // bn
    piece = rows // npieces
    out = jax.ShapeDtypeStruct((width // TILE, piece, TILE), F32)
    return pl.pallas_call(
        functools.partial(product_kernel, nblk, chunk * (width // TILE), tpb),
        out_shape=[out] * npieces,
        grid_spec=pltpu.PrefetchScalarGridSpec(
            num_scalar_prefetch=2,
            grid=(steps,),
            in_specs=[
                pl.BlockSpec((rows, depth), lambda i, o, m: (0, 0), pipeline_mode=pl.Buffered(1)),
                pl.BlockSpec((depth, bn), lambda i, o, m: (0, chunk * steps + i)),
            ],
            out_specs=[pl.BlockSpec((tpb, piece, TILE), lambda i, o, m: (i, 0, 0))] * npieces,
            scratch_shapes=[
                pltpu.VMEM((rows, depth), BF16),
                pltpu.VMEM((rows, depth), BF16),
                pltpu.VMEM((depth, bn), BF16),
                pltpu.VMEM((depth, bn), BF16),
            ],
        ),
        cost_estimate=pl.CostEstimate(
            flops=6 * rows * depth * width,
            bytes_accessed=4 * (rows * depth + depth * width + rows * width),
            transcendentals=0,
        ),
        compiler_params=pltpu.CompilerParams(vmem_limit_bytes=56 * 2**20),
        name="product",
    )(offsets, mask, amps, integrals)


def gather_kernel(idx_ref, x_ref, o_ref):
    n = o_ref.shape[0]
    base = pl.program_id(0) * n

    @pl.loop(0, n // 16)
    def _(i):
        for u in range(16):
            k = i * 16 + u
            o_ref[pl.ds(k, 1), :] = x_ref[pl.ds(idx_ref[base + k], 1), :]


def gather_units(units, idx):
    n = units.shape[0]
    bn = min(1024, n)
    return pl.pallas_call(
        gather_kernel,
        out_shape=jax.ShapeDtypeStruct(units.shape, F32),
        grid_spec=pltpu.PrefetchScalarGridSpec(
            num_scalar_prefetch=1,
            grid=(n // bn,),
            in_specs=[pl.BlockSpec(units.shape, lambda i, s: (0, 0), pipeline_mode=pl.Buffered(1))],
            out_specs=pl.BlockSpec((bn, TILE), lambda i, s: (i, 0)),
        ),
        compiler_params=pltpu.CompilerParams(vmem_limit_bytes=24 * 2**20),
        name="gather_units",
    )(idx, units)


def finish_kernel(tiles, tpb, idx_ref, mask_ref, got_ref, den_ref, cyc_ref, upd_ref, term_ref, moved, c_hi, c_lo):
    rows = den_ref.shape[0]
    k = pl.program_id(0)

    @pl.loop(0, rows // 8)
    def _(i):
        for u in range(8):
            r = i * 8 + u
            for t in range(tpb):
                q = idx_ref[r * tiles + k * tpb + t]
                moved[t, pl.ds(r, 1), :] = got_ref[pl.ds(q, 1), :]

    for u in range(tpb):
        for s in range(tpb):
            at = (pl.ds(u * TILE, TILE), pl.ds(s * TILE, TILE))
            hi, lo = split(cyc_ref[at] * mask_ref[k * tpb + u, s].astype(F32))
            c_hi[at] = hi
            c_lo[at] = lo
    upd = jnp.concatenate([moved[t] for t in range(tpb)], axis=1) / den_ref[...]
    upd_ref[...] = upd
    hi, lo = split(upd)
    term_ref[...] = dot(hi, c_hi[...]) + dot(lo, c_hi[...]) + dot(hi, c_lo[...])


def finish(got, inv, denominators, cycle_tiles, cycle_mask):
    rows, cols = denominators.shape
    rb = cycle_tiles.shape[1]
    out = jax.ShapeDtypeStruct((rows, cols), F32)
    block = pl.BlockSpec((rows, rb), lambda i, s, m: (0, i))
    return pl.pallas_call(
        functools.partial(finish_kernel, cols // TILE, rb // TILE),
        out_shape=[out, out],
        grid_spec=pltpu.PrefetchScalarGridSpec(
            num_scalar_prefetch=2,
            grid=(cols // rb,),
            in_specs=[
                pl.BlockSpec(got.shape, lambda i, s, m: (0, 0), pipeline_mode=pl.Buffered(1)),
                block,
                pl.BlockSpec((rb, rb), lambda i, s, m: (i, 0)),
            ],
            out_specs=[block, block],
            scratch_shapes=[
                pltpu.VMEM((rb // TILE, rows, TILE), F32),
                pltpu.VMEM((rb, rb), BF16),
                pltpu.VMEM((rb, rb), BF16),
            ],
        ),
        compiler_params=pltpu.CompilerParams(vmem_limit_bytes=40 * 2**20),
        name="finish",
    )(inv, cycle_mask, got, denominators, cycle_tiles)


def routes(destination, nrow, ncol):
    local_rows, local_tiles = destination.shape
    vt = local_tiles * ncol
    units = local_rows * local_tiles
    half = local_rows // 2
    tc = local_tiles // CHUNKS
    flat = destination.reshape(2, half, CHUNKS, tc).transpose(2, 0, 3, 1).reshape(-1)
    out_row = flat // vt
    out_tile = flat % vt
    owner = out_row // local_rows * ncol + out_tile // local_tiles
    place = out_row % local_rows * local_tiles + out_tile % local_tiles
    iota = lax.iota(jnp.int32, units)
    key, order = lax.sort((owner * units + place, iota), num_keys=1, is_stable=False)
    ndev = nrow * ncol
    places = (key % units).astype(F32).reshape(ndev, units // ndev)
    got_place = lax.all_to_all(places, ("row", "col"), split_axis=0, concat_axis=0, tiled=True)
    _, inv = lax.sort((got_place.reshape(-1).astype(jnp.int32), iota), num_keys=1, is_stable=False)
    return order, inv


def body(amplitudes, integrals, integral_mask, denominators, cycle_tiles, cycle_mask, destination):
    nrow = lax.axis_size("row")
    ncol = lax.axis_size("col")
    me = lax.axis_index("row")
    amps = lax.all_gather(amplitudes, "col", axis=0, tiled=True)
    order, inv = routes(destination, nrow, ncol)
    local_rows = destination.shape[0]
    half = local_rows // 2
    pieces = []
    if nrow == 4:
        up = [(i, (i + 1) % nrow) for i in range(nrow)]
        down = [(i, (i - 1) % nrow) for i in range(nrow)]
        offsets = jnp.stack([(me + d) % nrow for d in (2, 1, 3, 0)]).astype(jnp.int32)
        sent, landed = [], []
        for c in range(CHUNKS):
            if c >= 2:
                after = sent[c - 2] + (landed[c - 3] if c >= 3 else [])
                offsets = lax.optimization_barrier([offsets] + after)[0]
            far_a, far_b, up_a, up_b, dn_a, dn_b, own_a, own_b = product(
                amps, integrals, integral_mask, offsets, c, nrow, 2 * nrow)
            in_a = lax.ppermute(far_a, "row", up)
            in_b = lax.ppermute(far_b, "row", down)
            direct_b = lax.ppermute(up_b, "row", up)
            direct_a = lax.ppermute(dn_a, "row", down)
            next_a, next_b = up_a + in_a, dn_b + in_b
            sum_a = lax.ppermute(next_a, "row", up)
            sum_b = lax.ppermute(next_b, "row", down)
            sent.append([next_a, next_b, direct_a, direct_b])
            landed.append([sum_a, sum_b])
            pieces.append(own_a + direct_a + sum_a)
            pieces.append(own_b + direct_b + sum_b)
    else:
        offsets = lax.iota(jnp.int32, nrow)
        for c in range(CHUNKS):
            (part,) = product(amps, integrals, integral_mask, offsets, c, nrow, 1)
            summed = lax.psum_scatter(part, "row", scatter_dimension=1, tiled=True)
            pieces.append(summed[:, :half])
            pieces.append(summed[:, half:])
    units = jnp.concatenate([p.reshape(-1, TILE) for p in pieces], axis=0)
    sending = gather_units(units, order)
    ndev = nrow * ncol
    got = lax.all_to_all(sending.reshape(ndev, -1, TILE), ("row", "col"), split_axis=0, concat_axis=0, tiled=True)
    return tuple(finish(got.reshape(-1, TILE), inv, denominators, cycle_tiles, cycle_mask))


def solution(mesh):
    return jax.shard_map(
        body,
        mesh=mesh,
        in_specs=(
            P("col", "row"),
            P("row", "col"),
            P("row", "col"),
            P("row", "col"),
            P("col", None),
            P("col", None),
            P("row", "col"),
        ),
        out_specs=(P("row", "col"), P("row", "col")),
        check_vma=False,
    )
```
